32 devices in a mesh: tmpl: 4 (over y, core), seq: 2 (over x), tp: 4 (over z).
Axes of the slice: x: 2, y: 2, z: 4, core: 2. Of those that a mesh axis runs over, the one named last changes fastest.
Arguments:
- tokens: bfloat16 [3072, 5376], P(('tmpl', 'seq', 'tp')), parts along dimension 0, may hold values from -6 to 6
- lengths: int32 [8], P('tmpl'), parts along dimension 0, may hold values from 1 to 384, as said below
- input_gain: float32 [5376], replicated, may hold values from 0.1 to 1.9
- query_proj: bfloat16 [5376, 512], P(None, 'tp'), may hold values from -0.078125 to 0.078125
- key_value: bfloat16 [5376, 1024], P(None, 'tp'), may hold values from -0.078125 to 0.078125
- query_gain: float32 [128], replicated, may hold values from 0.5 to 20, as said below
- key_gain: float32 [128], replicated, may hold values from 0.5 to 6, as said below
- window_cache: bfloat16 [4096, 1024], P(('tmpl', 'seq'), 'tp'), parts along dimension 0, may hold values from -6 to 6
- output_proj: bfloat16 [512, 5376], P('tp', 'seq'), may hold values from -0.25 to 0.25
- post_gain: float32 [5376], replicated, may hold values from 0.1 to 1.9
Outputs:
- layer_out: bfloat16 [3072, 5376], P(('tmpl', 'seq', 'tp')), parts along dimension 0
The draws below stay inside these ranges and needn't reach their ends.
There are 4 independent parts, one for each index of `tmpl`. The reference program is written for one: setup_inputs(seed, part) draws one part's arguments, and reference() takes and returns one part's arrays. A program takes and returns all parts, laid end to end along the dimension named above; an argument that names none is the same for every part. Nothing has to cross between parts.
Inputs may be any that keep to these rules, and one draw needn't show every extreme that they name: The template's live slab tokens fill the first lengths[s] slots of seq index s, in order of s; one entry equals 384. `query_gain`: positive entries. `key_gain`: positive entries.
All inputs are finite; a program needn't handle non-finite values.
Results may differ from the reference program's by a relative error of at most 0.018.
The reference program's roundings to bfloat16 on the way (of `normed`, `queries`, `key_rows` and `head_out`) count: a program that leaves them out, or rounds other values in their place, can miss the bound.
Values may be sent and summed in bfloat16 or wider, within the bound.
A program may use at most 64 MiB of HBM per device.

```python
import math
import jax
import jax.numpy as jnp
from jax import lax

D = 5376
HD = 128
WIN = 1024
PREFIX = 32768
SLAB_DEV = 384
HEADS = 4
KV_HEADS = 4
SLOTS = 768
N_SEQ = 2


def gain_table(key, salt, low_end, high_end):
    uniform_draw = jax.random.uniform(jax.random.fold_in(key, salt), (HD,), jnp.float32)
    return jnp.exp(math.log(low_end) + uniform_draw * (math.log(high_end) - math.log(low_end)))


def draw_query_gain(key, part):
    return gain_table(key, 11, 0.5, 2.0)


def draw_key_gain(key, part):
    return gain_table(key, 12, 0.5, 2.0)


def draw_lengths(key, part):
    shard_index = jnp.arange(N_SEQ, dtype=jnp.int32)
    first_pick = jax.random.randint(jax.random.fold_in(key, 31), (N_SEQ,), 1, SLAB_DEV + 1)
    second_pick = jax.random.randint(jax.random.fold_in(key, 32), (N_SEQ,), 1, SLAB_DEV + 1)
    others = jnp.minimum(first_pick, second_pick).astype(jnp.int32)
    base_pick = jax.random.randint(jax.random.fold_in(key, 33), (), 0, SLAB_DEV - 1)
    tagged = (1 + (base_pick + part) % (SLAB_DEV - 1)).astype(jnp.int32)
    place = (jax.random.randint(jax.random.fold_in(key, 37), (), 0, N_SEQ) + part) % N_SEQ
    marked = (place + 1) % N_SEQ
    result = jnp.where(shard_index == place, SLAB_DEV, jnp.where(shard_index == marked, tagged, others))
    return result.astype(jnp.int32)


def draw_window_cache(key, part):
    cache_width = KV_HEADS * 2 * HD
    noise_draw = jnp.clip(jax.random.normal(jax.random.fold_in(key, 21), (WIN, cache_width), jnp.float32), -6.0, 6.0)
    return noise_draw.astype(jnp.bfloat16)


def shard_levels(key, shape, shards, low, top_value):
    def one(position, shards_of):
        draws = jax.random.uniform(jax.random.fold_in(jax.random.fold_in(key, 6), position), (shards_of,), jnp.float32, low / len(shards), top_value / len(shards))
        return jnp.repeat(jnp.exp(draws), shape[position] // shards_of).reshape((-1,) + (1,) * (len(shape) - position - 1))

    gain = one(*shards[0])
    for cut in shards[1:]:
        gain = gain * one(*cut)
    return gain


def scatter_about(rng, extent, width, bound, shards=(), held_as=jnp.bfloat16):
    drawn = jax.random.normal(rng, extent, jnp.float32) * width
    if len(shards) > 0:
        drawn = shard_levels(rng, extent, shards, -0.22, 0.18) * drawn
    return jnp.clip(drawn, min=-bound, max=bound).astype(held_as)


def setup_inputs(seed: int = 0, part: int = 0) -> dict:
    splits = jax.random.split(jax.random.key(seed), 11)
    part_keys = jax.random.split(jax.random.fold_in(splits[10], part), 11)
    return {
        "tokens": scatter_about(part_keys[0], (SLOTS, D), 1.0, 6.0, ((0, 8),)),
        "lengths": draw_lengths(jax.random.fold_in(jax.random.fold_in(splits[10], part), 71), part),
        "input_gain": jnp.clip(1.0 + 0.18 * jax.random.normal(splits[2], (D,), jnp.float32), 0.1, 1.9),
        "query_proj": scatter_about(splits[3], (D, HEADS * HD), D ** -0.5, 0.078125, ((1, 4),)),
        "key_value": scatter_about(splits[4], (D, KV_HEADS * 2 * HD), D ** -0.5, 0.078125, ((1, 4),)),
        "query_gain": draw_query_gain(jax.random.fold_in(splits[10], 71), part),
        "key_gain": draw_key_gain(jax.random.fold_in(splits[10], 71), part),
        "window_cache": draw_window_cache(jax.random.fold_in(jax.random.fold_in(splits[10], part), 71), part),
        "output_proj": scatter_about(splits[8], (HEADS * HD, D), (HEADS * HD) ** -0.5, 0.25, ((0, 4), (1, 2))),
        "post_gain": jnp.clip(1.0 + 0.18 * jax.random.normal(splits[9], (D,), jnp.float32), 0.1, 1.9),
    }


EPSILON = 1e-06
ROPE_BASE = 10000.0
QUERY_SCALE = 168.0 ** (-0.5)
MASKED = -1e+30

def normalize(values, scale_gain):
    values = values.astype(jnp.float32)
    return values * lax.rsqrt(lax.optimization_barrier(jnp.mean(values * values, axis=-1, keepdims=True)) + EPSILON) * scale_gain

def rotate(values, positions):
    half_width = values.shape[-1] // 2
    frequency = jnp.power(ROPE_BASE, -2.0 * jnp.arange(half_width, dtype=jnp.float32) / values.shape[-1])
    angles = positions.astype(jnp.float32)[:, None] * frequency[None, :]
    cosine_table = jnp.cos(angles)
    sine_table = jnp.sin(angles)
    first_half = values[:, :half_width]
    second_half = values[:, half_width:]
    return jnp.concatenate([first_half * cosine_table - second_half * sine_table, second_half * cosine_table + first_half * sine_table], axis=1)

def reference(tokens, lengths, input_gain, query_proj, key_value, query_gain, key_gain, window_cache, output_proj, post_gain):
    normed = normalize(tokens, input_gain).astype(jnp.bfloat16)
    query_raw = jnp.dot(normed, query_proj, preferred_element_type=jnp.float32)
    kv_raw = jnp.dot(normed, key_value, preferred_element_type=jnp.float32)
    offsets = (jnp.cumsum(lengths) - lengths).astype(jnp.int32)
    slot_index = jnp.arange(SLAB_DEV, dtype=jnp.int32)
    positions = (PREFIX + offsets[:, None] + slot_index[None, :]).reshape(-1).astype(jnp.int32)
    live_rows = (slot_index[None, :] < lengths[:, None]).reshape(-1)
    cache_position = (PREFIX - WIN + jnp.arange(WIN, dtype=jnp.int32)).astype(jnp.int32)
    key_position = jnp.concatenate([cache_position, positions])
    key_live = jnp.concatenate([jnp.ones((WIN,), dtype=bool), live_rows])
    allowed = key_live[None, :] & (key_position[None, :] <= positions[:, None]) & (key_position[None, :] > positions[:, None] - WIN)
    projection = jnp.zeros((tokens.shape[0], tokens.shape[1]), jnp.float32)
    for head_index in range(HEADS):
        queries = (rotate(normalize(query_raw[:, head_index * HD:(head_index + 1) * HD], query_gain), positions) * QUERY_SCALE).astype(jnp.bfloat16)
        new_keys = rotate(normalize(kv_raw[:, 2 * head_index * HD:(2 * head_index + 1) * HD], key_gain), positions).astype(jnp.bfloat16)
        new_values = kv_raw[:, (2 * head_index + 1) * HD:(2 * head_index + 2) * HD].astype(jnp.bfloat16)
        key_rows = jnp.concatenate([window_cache[:, 2 * head_index * HD:(2 * head_index + 1) * HD], new_keys], axis=0)
        value_rows = jnp.concatenate([window_cache[:, (2 * head_index + 1) * HD:(2 * head_index + 2) * HD], new_values], axis=0)
        scores = jnp.dot(queries, key_rows.T, preferred_element_type=jnp.float32)
        scores = jnp.where(allowed, scores, MASKED)
        row_max = lax.optimization_barrier(jnp.max(scores, axis=1, keepdims=True))
        weights = jnp.where(allowed, jnp.exp(scores - row_max), 0.0)
        row_sum = lax.optimization_barrier(jnp.sum(weights, axis=1))
        head_out = jnp.dot(weights.astype(jnp.bfloat16), value_rows, preferred_element_type=jnp.float32)
        head_out = head_out / jnp.where(live_rows, row_sum, 1.0)[:, None]
        head_out = jnp.where(live_rows[:, None], head_out, 0.0).astype(jnp.bfloat16)
        head_term = jnp.dot(head_out, output_proj[head_index * HD:(head_index + 1) * HD], preferred_element_type=jnp.float32).astype(jnp.bfloat16)
        projection = projection + lax.optimization_barrier(head_term).astype(jnp.float32)
    post_norm = normalize(projection, post_gain)
    return (tokens.astype(jnp.float32) + post_norm).astype(jnp.bfloat16)
```

```python
import functools

import jax
import jax.numpy as jnp
from jax import lax
from jax.experimental import pallas as pl
from jax.experimental.pallas import tpu as pltpu
from jax.sharding import PartitionSpec as P

WIN = 1024
PREFIX = 32768
EPSILON = 1e-06
ROPE_BASE = 10000.0
QUERY_SCALE = 168.0 ** (-0.5)
MASKED = -1e30
F32 = jnp.float32
BF16 = jnp.bfloat16
MESH = pl.DeviceIdType.MESH


def chunk_of(width, limit):
    best = 128
    for c in range(128, limit + 1, 128):
        if width % c == 0:
            best = c
    return best


def flat(v):
    shape = (v.shape[0] * v.shape[1], v.shape[2])
    if v.shape[1] % 16 == 0:
        return v.reshape(shape)
    return v.astype(F32).reshape(shape).astype(v.dtype)


def kernel(
    T, S, N, S2,
    lengths, tokens, wq_hbm, wkv_hbm, cache_hbm, oproj_hbm,
    igain, pgain, qgain, kgain, cos_t, sin_t,
    out_ref,
    xbuf, nbuf, wq, wkv, cbuf, og, q_all, kv_all, q_snd, kv_snd, hsnd, ho, proj,
    lsem, ssem, hssem,
    r_x, r_c, r_w, r_oz, r_op, r_q, r_kv, r_kvx, r_h, r_own,
):
    t, s, z = lax.axis_index("tmpl"), lax.axis_index("seq"), lax.axis_index("tp")
    h = N // 2
    p, b = z // h, z % h
    zp = (z + h) % N
    R, D = tokens.shape
    HW = wq_hbm.shape[1]
    C = cache_hbm.shape[0]
    DE = D // (T * S2)
    OR = oproj_hbm.shape[0] // T
    DC = oproj_hbm.shape[1]
    tc = t + 1 - 2 * (t % 2)
    par = t % 2
    ys = [(t + 2 * k) % T for k in range(1, T // 2)]
    xs = [(s + k) % S for k in range(1, S)]
    sg, sb = (s // S2) * S2, s % S2
    x2 = [(sb + k) % S2 for k in range(1, S2)]
    zs = [(z + k) % N for k in range(1, N)]

    pending = []

    def send(src, dst, rsem, dev):
        c = pltpu.make_async_remote_copy(
            src_ref=src, dst_ref=dst, send_sem=ssem.at[len(pending)], recv_sem=rsem,
            device_id=dev, device_id_type=MESH,
        )
        c.start()
        pending.append(c)

    def arrived(dst, rsem):
        pltpu.make_async_remote_copy(
            src_ref=dst, dst_ref=dst, send_sem=ssem.at[0], recv_sem=rsem,
            device_id={"tp": zp}, device_id_type=MESH,
        ).wait_recv()

    loc = [
        pltpu.make_async_copy(tokens, xbuf.at[b], lsem.at[0]),
        pltpu.make_async_copy(wq_hbm, wq.at[0], lsem.at[1]),
        pltpu.make_async_copy(wkv_hbm, wkv.at[0], lsem.at[2]),
        pltpu.make_async_copy(cache_hbm, cbuf.at[s], lsem.at[3]),
        pltpu.make_async_copy(
            oproj_hbm.at[pl.ds(pl.multiple_of(t * OR, OR), OR)], og.at[s, t, z], lsem.at[4]
        ),
    ]
    for c in loc:
        c.start()

    barrier = pltpu.get_barrier_semaphore()
    peers = (
        [{"tp": k} for k in zs] + [{"seq": k} for k in xs]
        + [{"tmpl": k} for k in ys] + [{"tmpl": tc}]
    )
    for dev in peers:
        pl.semaphore_signal(barrier, inc=1, device_id=dev, device_id_type=MESH)
    pl.semaphore_wait(barrier, len(peers))

    def piece(e_t, e_s):
        return pl.ds(pl.multiple_of((e_t * S2 + e_s) * DE, DE), DE)

    wset = ((1, wkv_hbm, wkv), (0, wq_hbm, wq))
    for a, src, buf in wset:
        send(src.at[piece(t, sb)], buf.at[1, piece(t, sb)], r_own.at[a], {"tp": zp})
    for k in range(1, h):
        send(tokens, xbuf.at[b], r_x.at[b], {"tp": p * h + (b + k) % h})
    for k in zs:
        send(
            oproj_hbm.at[pl.ds(pl.multiple_of(t * OR, OR), OR)], og.at[s, t, z],
            r_oz.at[z], {"tp": k},
        )
    for k in xs:
        send(cache_hbm, cbuf.at[s], r_c.at[s], {"seq": k})

    RB = 16 if R % 16 == 0 else 8
    KC = chunk_of(D, 1024)

    def norm_rows(slot):
        def body(i, carry):
            rows = pl.ds(pl.multiple_of(i * RB, RB), RB)
            v = xbuf[slot, rows, :].astype(F32)
            inv = lax.rsqrt(jnp.sum(v * v, axis=1, keepdims=True) * (1.0 / D) + EPSILON)
            nbuf[slot, rows, :] = (v * inv * igain[...]).astype(BF16)
            return carry

        lax.fori_loop(0, R // RB, body, 0)

    def head_norm(v, gain):
        inv = lax.rsqrt(jnp.mean(v * v, axis=1, keepdims=True) + EPSILON)
        return v * inv * gain

    def project(slot, j):
        def body(i, acc):
            ks = pl.ds(pl.multiple_of(i * KC, KC), KC)
            xv = nbuf[slot, :, ks]
            return (
                acc[0] + jnp.dot(xv, wq[j, ks, :], preferred_element_type=F32),
                acc[1] + jnp.dot(xv, wkv[j, ks, :], preferred_element_type=F32),
            )

        qr, kv = lax.fori_loop(
            0, D // KC, body, (jnp.zeros((R, HW), F32), jnp.zeros((R, 2 * HW), F32))
        )
        co, si = cos_t[slot], sin_t[slot]

        def rope(u):
            return u * co + pltpu.roll(u, HW // 2, 1) * si

        q = (rope(head_norm(qr, qgain[...])) * QUERY_SCALE).astype(BF16)
        k = rope(head_norm(kv[:, :HW], kgain[...])).astype(BF16)
        return q, jnp.concatenate([k, kv[:, HW:].astype(BF16)], axis=1)

    def own_head(slot):
        q, kv = project(slot, 0)
        n = p * h + slot
        q_all[n] = q
        kv_all[s, n] = kv
        for k in xs:
            send(kv_all.at[s, n], kv_all.at[s, n], r_kvx.at[s, n], {"seq": k})

    def other_head(slot):
        q, kv = project(slot, 1)
        n = p * h + slot
        q_snd[slot] = q
        kv_snd[slot] = kv
        send(kv_snd.at[slot], kv_all.at[s, n], r_kv.at[n], {"tp": zp})
        send(q_snd.at[slot], q_all.at[n], r_q.at[n], {"tp": zp})

    loc[0].wait()
    norm_rows(b)
    loc[1].wait()
    loc[2].wait()
    own_head(b)

    for a, src, buf in wset:
        pc = buf.at[1, piece(t, sb)]
        arrived(pc, r_own.at[a])
        for k in x2:
            send(pc, pc, r_w.at[a, t, sb], {"seq": sg + k})
        for k in ys:
            send(pc, pc, r_w.at[a, t, sb], {"tmpl": k})
        send(pc, pc, r_w.at[a, t, sb], {"tmpl": tc})
    for a, src, buf in wset:
        for k2 in x2:
            pc = buf.at[1, piece(t, k2)]
            arrived(pc, r_w.at[a, t, k2])
            for k in ys:
                send(pc, pc, r_w.at[a, t, k2], {"tmpl": k})
            send(pc, pc, r_w.at[a, t, k2], {"tmpl": tc})
    loc[4].wait()
    for k in zs:
        arrived(og.at[s, t, k], r_oz.at[k])

    def out_send(ps, pt, over_y, over_x):
        pc = og.at[ps, pt]
        if over_x:
            for k in xs:
                send(pc, pc, r_op.at[ps, pt], {"seq": k})
        if over_y:
            for k in ys:
                send(pc, pc, r_op.at[ps, pt], {"tmpl": k})
        send(pc, pc, r_op.at[ps, pt], {"tmpl": tc})

    for a, src, buf in wset:
        for k in ys:
            for k2 in range(S2):
                ks = (sb + k2) % S2
                pc = buf.at[1, piece(k, ks)]
                arrived(pc, r_w.at[a, k, ks])
                send(pc, pc, r_w.at[a, k, ks], {"tmpl": tc})
    out_send(s, t, True, True)

    for k in range(1, h):
        slot = (b + k) % h
        arrived(xbuf.at[slot], r_x.at[slot])
        norm_rows(slot)
        own_head(slot)
    for a, src, buf in wset:
        for k in range(T // 2):
            kt = (1 - par) + 2 * k
            for ks in range(S2):
                arrived(buf.at[1, piece(kt, ks)], r_w.at[a, kt, ks])
    for k in range(h):
        other_head((b + k) % h)

    for k in ys:
        arrived(og.at[s, k], r_op.at[s, k])
        out_send(s, k, False, True)

    op = 1 - p
    for i in range(h):
        n = op * h + i
        arrived(kv_all.at[s, n], r_kv.at[n])
        for k in xs:
            send(kv_all.at[s, n], kv_all.at[s, n], r_kvx.at[s, n], {"seq": k})
    for i in range(h):
        n = op * h + i
        arrived(q_all.at[n], r_q.at[n])
    for k in xs:
        for kt in range(T // 2):
            ot = par + 2 * kt
            arrived(og.at[k, ot], r_op.at[k, ot])
            out_send(k, ot, False, False)
    loc[3].wait()
    for k in xs:
        arrived(cbuf.at[k], r_c.at[k])
        for n in range(N):
            arrived(kv_all.at[k, n], r_kvx.at[k, n])

    lens = [lengths[k] for k in range(S)]
    offs = []
    total = jnp.int32(0)
    for k in range(S):
        offs.append(total)
        total = total + lens[k]
    own_off = jnp.int32(0)
    own_len = jnp.int32(0)
    for k in range(S):
        own_off = own_off + jnp.where(s == k, offs[k], 0)
        own_len = own_len + jnp.where(s == k, lens[k], 0)

    def attend(d, carry):
        n = lax.rem(z + d, N)
        q = q_all[n]
        slot_c = n * R + lax.broadcasted_iota(jnp.int32, (R, 1), 0)
        pos = PREFIX + own_off + slot_c
        scores, allow, values = [], [], []
        for k in range(S):
            cb = cbuf[k]
            sc = lax.dot_general(
                q, cb[:, :HW], (((1,), (1,)), ((), ())), preferred_element_type=F32
            )
            kp = PREFIX - WIN + k * C + lax.broadcasted_iota(jnp.int32, (1, C), 1)
            ok = (kp <= pos) & (kp > pos - WIN)
            scores.append(jnp.where(ok, sc, MASKED))
            allow.append(ok)
            values.append(cb[:, HW:])
            kv = flat(kv_all[k])
            sc = lax.dot_general(
                q, kv[:, :HW], (((1,), (1,)), ((), ())), preferred_element_type=F32
            )
            j = lax.broadcasted_iota(jnp.int32, (1, N * R), 1)
            kp = PREFIX + offs[k] + j
            ok = (kp <= pos) & (kp > pos - WIN) & (j < lens[k])
            scores.append(jnp.where(ok, sc, MASKED))
            allow.append(ok)
            values.append(kv[:, HW:])
        top = functools.reduce(
            jnp.maximum, [jnp.max(v, axis=1, keepdims=True) for v in scores]
        )
        row_sum = jnp.zeros((R, 1), F32)
        acc = jnp.zeros((R, HW), F32)
        for sc, ok, vv in zip(scores, allow, values):
            w = jnp.where(ok, jnp.exp(sc - top), 0.0)
            row_sum = row_sum + jnp.sum(w, axis=1, keepdims=True)
            acc = acc + jnp.dot(w.astype(BF16), vv, preferred_element_type=F32)
        live = slot_c < own_len
        res = acc / jnp.where(live, row_sum, 1.0)
        hsnd[n] = jnp.where(live, res, 0.0).astype(BF16)

        @pl.when(d < N)
        def _():
            pltpu.make_async_remote_copy(
                src_ref=hsnd.at[n], dst_ref=ho.at[z], send_sem=hssem.at[n],
                recv_sem=r_h.at[z], device_id={"tp": n}, device_id_type=MESH,
            ).start()

        return carry

    lax.fori_loop(1, N + 1, attend, 0)
    ho[z] = hsnd[z]

    for k in range(S):
        for kt in range(T // 2):
            ot = (1 - par) + 2 * kt
            arrived(og.at[k, ot], r_op.at[k, ot])
    for k in zs:
        arrived(ho.at[k], r_h.at[k])

    CC = chunk_of(DC, 1024)

    for k in range(S):
        def cols(i, carry):
            cs = pl.ds(pl.multiple_of(i * CC, CC), CC)
            acc = jnp.zeros((R, CC), F32)
            for g in range(N):
                w = jnp.concatenate([og[k, kt, g, :, cs] for kt in range(T)], axis=0)
                acc = acc + jnp.dot(ho[g], w, preferred_element_type=F32).astype(BF16).astype(F32)
            proj[:, pl.ds(pl.multiple_of(k * DC + i * CC, 128), CC)] = acc
            return carry

        lax.fori_loop(0, DC // CC, cols, 0)

    def finish(i, carry):
        rows = pl.ds(pl.multiple_of(i * RB, RB), RB)
        v = proj[rows, :]
        inv = lax.rsqrt(jnp.sum(v * v, axis=1, keepdims=True) * (1.0 / D) + EPSILON)
        out_ref[rows, :] = (xbuf[b, rows, :].astype(F32) + v * inv * pgain[...]).astype(BF16)
        return carry

    lax.fori_loop(0, R // RB, finish, 0)

    for c in pending:
        c.wait_send()
    for k in zs:
        pltpu.make_async_remote_copy(
            src_ref=hsnd.at[k], dst_ref=ho.at[z], send_sem=hssem.at[k],
            recv_sem=r_h.at[z], device_id={"tp": k}, device_id_type=MESH,
        ).wait_send()


def shards(
    T, S, N,
    tokens, lengths, input_gain, query_proj, key_value, query_gain, key_gain,
    window_cache, output_proj, post_gain,
):
    R, D = tokens.shape
    HW = query_proj.shape[1]
    C = window_cache.shape[0]
    h = N // 2
    S2 = max(d for d in range(1, S + 1) if S % d == 0 and D % (16 * T * d) == 0)
    s, z = lax.axis_index("seq"), lax.axis_index("tp")
    own_offset = jnp.sum(jnp.where(jnp.arange(S, dtype=jnp.int32) < s, lengths, 0))
    slot = (z // h) * (h * R) + jnp.arange(h * R, dtype=jnp.int32)
    positions = PREFIX + own_offset + slot
    half = HW // 2
    freq = jnp.power(ROPE_BASE, -2.0 * jnp.arange(half, dtype=F32) / HW)
    angles = positions.astype(F32)[:, None] * freq[None, :]
    co, si = jnp.cos(angles), jnp.sin(angles)
    cos_t = jnp.concatenate([co, co], axis=1).reshape(h, R, HW)
    sin_t = jnp.concatenate([-si, si], axis=1).reshape(h, R, HW)
    OR, DC = output_proj.shape[0] // T, output_proj.shape[1]
    w_sends = 2 * (1 + (S2 - 1 + T // 2) + (S2 - 1) * (T // 2) + (T // 2 - 1) * S2)
    o_sends = (N - 1) + (T // 2 - 1) + (T // 2) * (S - 1) + S * (T // 2)
    sends = w_sends + o_sends + (h - 1) + (S - 1) + N * (S - 1) + 2 * h
    vm = pl.BlockSpec(memory_space=pltpu.VMEM)
    hb = pl.BlockSpec(memory_space=pl.ANY)
    dma = pltpu.SemaphoreType.DMA
    return pl.pallas_call(
        functools.partial(kernel, T, S, N, S2),
        out_shape=jax.ShapeDtypeStruct((R, D), BF16),
        in_specs=[pl.BlockSpec(memory_space=pltpu.SMEM), hb, hb, hb, hb, hb]
        + [vm] * 6,
        out_specs=vm,
        scratch_shapes=[
            pltpu.VMEM((h, R, D), BF16),
            pltpu.VMEM((h, R, D), BF16),
            pltpu.VMEM((2, D, HW), BF16),
            pltpu.VMEM((2, D, 2 * HW), BF16),
            pltpu.VMEM((S, C, 2 * HW), BF16),
            pltpu.VMEM((S, T, N, OR, DC), BF16),
            pltpu.VMEM((N, R, HW), BF16),
            pltpu.VMEM((S, N, R, 2 * HW), BF16),
            pltpu.VMEM((h, R, HW), BF16),
            pltpu.VMEM((h, R, 2 * HW), BF16),
            pltpu.VMEM((N, R, HW), BF16),
            pltpu.VMEM((N, R, HW), BF16),
            pltpu.VMEM((R, D), F32),
            dma((5,)), dma((sends,)), dma((N,)),
            dma((h,)), dma((S,)), dma((2, T, S2)), dma((N,)), dma((S, T)),
            dma((N,)), dma((N,)), dma((S, N)), dma((N,)), dma((2,)),
        ],
        compiler_params=pltpu.CompilerParams(
            collective_id=0, has_side_effects=True, vmem_limit_bytes=60 * 2**20
        ),
    )(
        lengths, tokens, query_proj, key_value, window_cache, output_proj,
        input_gain[None, :], post_gain[None, :], query_gain[None, :], key_gain[None, :],
        cos_t, sin_t,
    )


def solution(mesh):
    T, S, N = mesh.shape["tmpl"], mesh.shape["seq"], mesh.shape["tp"]
    return jax.shard_map(
        functools.partial(shards, T, S, N),
        mesh=mesh,
        in_specs=(
            P(("tmpl", "seq", "tp"), None),
            P("tmpl"),
            P(),
            P(None, "tp"),
            P(None, "tp"),
            P(),
            P(),
            P(("tmpl", "seq"), "tp"),
            P("tp", "seq"),
            P(),
        ),
        out_specs=P(("tmpl", "seq", "tp"), None),
        check_vma=False,
    )
```

```python
import functools

import jax
import jax.numpy as jnp
import numpy as np
from jax import lax
from jax.experimental import pallas as pl
from jax.experimental.pallas import tpu as pltpu
from jax.sharding import PartitionSpec as P

WIN = 1024
PREFIX = 32768
EPSILON = 1e-06
ROPE_BASE = 10000.0
QUERY_SCALE = 168.0 ** (-0.5)
MASKED = -1e30
F32 = jnp.float32
BF16 = jnp.bfloat16
MESH = pl.DeviceIdType.MESH


def chunk_of(width, limit):
    best = 128
    for c in range(128, limit + 1, 128):
        if width % c == 0:
            best = c
    return best


def flat(v):
    shape = (v.shape[0] * v.shape[1], v.shape[2])
    if v.shape[1] % 16 == 0:
        return v.reshape(shape)
    return v.astype(F32).reshape(shape).astype(v.dtype)


def kernel(
    T, S, N, S2, NC, NG,
    lengths, tokens, wq_hbm, wkv_hbm, cache_hbm, oproj_hbm,
    ig_hbm, pg_hbm, qgain, kgain, freq,
    out_ref,
    igs, pgs, igain, pgain, cos_t, sin_t, xbuf, nbuf, wq, wkv, cbuf, og, q_all, kv_all, q_snd, kv_snd, hsnd, ho, proj,
    lsem, ssem, hssem,
    r_x, r_c, r_w, r_oz, r_o, r_q, r_kv, r_kvx, r_h, r_own,
):
    t, s, z = lax.axis_index("tmpl"), lax.axis_index("seq"), lax.axis_index("tp")
    h = N // 2
    p, b = z // h, z % h
    zp = (z + h) % N
    R, D = tokens.shape
    HW = wq_hbm.shape[1]
    C = cache_hbm.shape[0]
    DE = D // (T * S2)
    OR = oproj_hbm.shape[0] // T
    DC = oproj_hbm.shape[1]
    tc = t + 1 - 2 * (t % 2)
    par = t % 2
    ys = [(t + 2 * k) % T for k in range(1, T // 2)]
    xs = [(s + k) % S for k in range(1, S)]
    sg, sb = (s // S2) * S2, s % S2
    x2 = [(sb + k) % S2 for k in range(1, S2)]
    zs = [(z + k) % N for k in range(1, N)]

    pending = []

    def queue(src, dst, rsem, dev):
        c = pltpu.make_async_remote_copy(
            src_ref=src, dst_ref=dst, send_sem=ssem.at[len(pending)], recv_sem=rsem,
            device_id=dev, device_id_type=MESH,
        )
        pending.append(c)
        return c

    def send(src, dst, rsem, dev):
        queue(src, dst, rsem, dev).start()

    def arrived(dst, rsem):
        pltpu.make_async_remote_copy(
            src_ref=dst, dst_ref=dst, send_sem=ssem.at[0], recv_sem=rsem,
            device_id={"tp": zp}, device_id_type=MESH,
        ).wait_recv()

    loc = [
        pltpu.make_async_copy(tokens, xbuf.at[b], lsem.at[0]),
        pltpu.make_async_copy(wq_hbm, wq.at[0], lsem.at[1]),
        pltpu.make_async_copy(wkv_hbm, wkv.at[0], lsem.at[2]),
        pltpu.make_async_copy(cache_hbm, cbuf.at[s], lsem.at[3]),
        pltpu.make_async_copy(
            oproj_hbm.at[pl.ds(pl.multiple_of(t * OR, OR), OR)], og.at[s, t, z], lsem.at[4]
        ),
        pltpu.make_async_copy(ig_hbm, igs, lsem.at[5]),
        pltpu.make_async_copy(pg_hbm, pgs, lsem.at[6]),
    ]
    for c in loc:
        c.start()

    barrier = pltpu.get_barrier_semaphore()
    peers = (
        [{"tp": k} for k in zs] + [{"seq": k} for k in xs]
        + [{"tmpl": k} for k in ys] + [{"tmpl": tc}]
    )
    for dev in peers:
        pl.semaphore_signal(barrier, inc=1, device_id=dev, device_id_type=MESH)
    pl.semaphore_wait(barrier, len(peers))

    DN = DE // NC

    def piece(e_t, e_s, c):
        return pl.ds(pl.multiple_of((e_t * S2 + e_s) * DE + c * DN, DN), DN)

    wset = [
        (c, a, src, buf)
        for c in range(NC)
        for a, src, buf in ((1, wkv_hbm, wkv), (0, wq_hbm, wq))
    ]
    w_first = [
        queue(
            src.at[piece(t, sb, c)], buf.at[1, piece(t, sb, c)],
            r_own.at[a, c], {"tp": zp},
        )
        for c, a, src, buf in wset
    ]
    rows_first = [
        queue(tokens, xbuf.at[b], r_x.at[b], {"tp": p * h + (b + k) % h})
        for k in range(1, h)
    ]

    @pl.when(par == 0)
    def _():
        for c in w_first + rows_first:
            c.start()

    @pl.when(par == 1)
    def _():
        for c in rows_first + w_first:
            c.start()

    for k in xs:
        send(cache_hbm, cbuf.at[s], r_c.at[s], {"seq": k})
    for k in zs:
        send(
            oproj_hbm.at[pl.ds(pl.multiple_of(t * OR, OR), OR)], og.at[s, t, z],
            r_oz.at[z], {"tp": k},
        )

    GN = N // NG
    gz, zl = z // GN, z % GN
    OH = OR // 2

    def op_full(ps, pt, g):
        return og.at[ps, pt, pl.ds(g * GN, GN)]

    def op_half(ps, pt, g, f):
        return og.at[ps, pt, pl.ds(g * GN, GN), pl.ds(f * OH, OH)]

    def out_own(j):
        g = (gz + j) % NG
        for k in range(1 if j == 0 else 0, GN):
            n = g * GN + (zl + k) % GN
            arrived(og.at[s, t, n], r_oz.at[n])
        pc = op_full(s, t, g)
        for k in xs:
            send(pc, pc, r_o.at[0, s, t, g], {"seq": k})
        for k in ys:
            send(pc, pc, r_o.at[0, s, t, g], {"tmpl": k})
        send(pc, pc, r_o.at[0, s, t, g], {"tmpl": tc})

    def out_second(j):
        g = (gz + j) % NG
        for kt in ys:
            pc = op_full(s, kt, g)
            arrived(pc, r_o.at[0, s, kt, g])
            hf = op_half(s, kt, g, 0)
            for k in xs:
                send(hf, hf, r_o.at[0, s, kt, g], {"seq": k})
            send(pc, pc, r_o.at[0, s, kt, g], {"tmpl": tc})
        for ks in xs:
            pc = op_full(ks, t, g)
            arrived(pc, r_o.at[0, ks, t, g])
            hf = op_half(ks, t, g, 1)
            for k in ys:
                send(hf, hf, r_o.at[1, ks, t, g], {"tmpl": k})
            send(pc, pc, r_o.at[0, ks, t, g], {"tmpl": tc})

    def out_third(j):
        g = (gz + j) % NG
        for ks in xs:
            for kt in ys:
                for f in range(2):
                    hf = op_half(ks, kt, g, f)
                    arrived(hf, r_o.at[f, ks, kt, g])
                    send(hf, hf, r_o.at[f, ks, kt, g], {"tmpl": tc})

    def out_last(j):
        g = (gz + j) % NG
        for i in range(S):
            for m in range(T // 2):
                ks, kt = (s + i) % S, (tc + 2 * m) % T
                if i and m:
                    for f in range(2):
                        arrived(op_half(ks, kt, g, f), r_o.at[f, ks, kt, g])
                else:
                    arrived(op_full(ks, kt, g), r_o.at[0, ks, kt, g])

    loc[4].wait()
    if GN == 1:
        out_own(0)

    lens = [lengths[k] for k in range(S)]
    offs = []
    total = jnp.int32(0)
    for k in range(S):
        offs.append(total)
        total = total + lens[k]
    own_off = jnp.int32(0)
    own_len = jnp.int32(0)
    for k in range(S):
        own_off = own_off + jnp.where(s == k, offs[k], 0)
        own_len = own_len + jnp.where(s == k, lens[k], 0)

    RB = 16 if R % 16 == 0 else 8
    KC = chunk_of(D, 1024)

    def norm_rows(slot):
        def body(i, carry):
            rows = pl.ds(pl.multiple_of(i * RB, RB), RB)
            v = xbuf[slot, rows, :].astype(F32)
            inv = lax.rsqrt(jnp.sum(v * v, axis=1, keepdims=True) * (1.0 / D) + EPSILON)
            nbuf[slot, rows, :] = (v * inv * igain[...]).astype(BF16)
            return carry

        lax.fori_loop(0, R // RB, body, 0)

    def head_norm(v, gain):
        inv = lax.rsqrt(jnp.mean(v * v, axis=1, keepdims=True) + EPSILON)
        return v * inv * gain

    def project(slot, j):
        def body(i, acc):
            ks = pl.ds(pl.multiple_of(i * KC, KC), KC)
            xv = nbuf[slot, :, ks]
            return (
                acc[0] + jnp.dot(xv, wq[j, ks, :], preferred_element_type=F32),
                acc[1] + jnp.dot(xv, wkv[j, ks, :], preferred_element_type=F32),
            )

        qr, kv = lax.fori_loop(
            0, D // KC, body, (jnp.zeros((R, HW), F32), jnp.zeros((R, 2 * HW), F32))
        )
        co, si = cos_t[slot], sin_t[slot]

        def rope(u):
            return u * co + pltpu.roll(u, HW // 2, 1) * si

        q = (rope(head_norm(qr, qgain[...])) * QUERY_SCALE).astype(BF16)
        k = rope(head_norm(kv[:, :HW], kgain[...])).astype(BF16)
        return q, jnp.concatenate([k, kv[:, HW:].astype(BF16)], axis=1)

    def own_head(slot):
        q, kv = project(slot, 0)
        n = p * h + slot
        q_all[n] = q
        kv_all[s, n] = kv
        for k in xs:
            send(kv_all.at[s, n], kv_all.at[s, n], r_kvx.at[s, n], {"seq": k})

    def other_head(slot):
        q, kv = project(slot, 1)
        n = p * h + slot
        q_snd[slot] = q
        kv_snd[slot] = kv
        send(kv_snd.at[slot], kv_all.at[s, n], r_kv.at[n], {"tp": zp})
        send(q_snd.at[slot], q_all.at[n], r_q.at[n], {"tp": zp})

    loc[5].wait()
    loc[6].wait()
    for k in range(D // 128):
        igain[0:1, k * 128 : (k + 1) * 128] = igs[k : k + 1, :]
        pgain[0:1, k * 128 : (k + 1) * 128] = pgs[k : k + 1, :]
    lane = lax.broadcasted_iota(jnp.int32, (R, HW), 1)
    for k in range(h):
        row = lax.broadcasted_iota(jnp.int32, (R, HW), 0)
        angle = (PREFIX + own_off + (p * h + k) * R + row).astype(F32) * freq[...]
        cos_t[k] = jnp.cos(angle)
        sine = jnp.sin(angle)
        sin_t[k] = jnp.where(lane < HW // 2, -sine, sine)
    loc[0].wait()
    norm_rows(b)
    loc[1].wait()
    loc[2].wait()
    own_head(b)

    def w_own(c, a, src, buf):
        pc = buf.at[1, piece(t, sb, c)]
        arrived(pc, r_own.at[a, c])
        for k in x2:
            send(pc, pc, r_w.at[a, t, sb, c], {"seq": sg + k})
        for k in ys:
            send(pc, pc, r_w.at[a, t, sb, c], {"tmpl": k})
        send(pc, pc, r_w.at[a, t, sb, c], {"tmpl": tc})

    def w_x(c, a, src, buf):
        for k2 in x2:
            pc = buf.at[1, piece(t, k2, c)]
            arrived(pc, r_w.at[a, t, k2, c])
            for k in ys:
                send(pc, pc, r_w.at[a, t, k2, c], {"tmpl": k})
            send(pc, pc, r_w.at[a, t, k2, c], {"tmpl": tc})

    def w_y(c, a, src, buf):
        for k in ys:
            for k2 in range(S2):
                ks = (sb + k2) % S2
                pc = buf.at[1, piece(k, ks, c)]
                arrived(pc, r_w.at[a, k, ks, c])
                send(pc, pc, r_w.at[a, k, ks, c], {"tmpl": tc})

    for i in range(NC + 1):
        if i < NC:
            for w in wset[2 * i : 2 * i + 2]:
                w_own(*w)
        if i == 0 and GN == 1:
            out_second(0)
        if i > 0:
            for w in wset[2 * i - 2 : 2 * i]:
                w_x(*w)
    for w in wset:
        w_y(*w)

    for k in range(1, h):
        slot = (b + k) % h
        arrived(xbuf.at[slot], r_x.at[slot])
        norm_rows(slot)
        own_head(slot)
    for c, a, src, buf in wset:
        for k in range(T // 2):
            kt = (1 - par) + 2 * k
            for ks in range(S2):
                arrived(buf.at[1, piece(kt, ks, c)], r_w.at[a, kt, ks, c])
    for k in range(h):
        other_head((b + k) % h)

    for j in range(1 if GN == 1 else 0, NG):
        out_own(j)

    op = 1 - p
    for i in range(h):
        n = op * h + i
        arrived(kv_all.at[s, n], r_kv.at[n])
        for k in xs:
            send(kv_all.at[s, n], kv_all.at[s, n], r_kvx.at[s, n], {"seq": k})
    for i in range(h):
        n = op * h + i
        arrived(q_all.at[n], r_q.at[n])
    for j in range(1 if GN == 1 else 0, NG):
        out_second(j)
    loc[3].wait()
    for k in xs:
        arrived(cbuf.at[k], r_c.at[k])
        for n in range(N):
            arrived(kv_all.at[k, n], r_kvx.at[k, n])

    def attend(d, carry):
        n = lax.rem(z + d, N)
        q = q_all[n]
        slot_c = n * R + lax.broadcasted_iota(jnp.int32, (R, 1), 0)
        pos = PREFIX + own_off + slot_c
        scores, allow, values = [], [], []
        for k in range(S):
            cb = cbuf[k]
            sc = lax.dot_general(
                q, cb[:, :HW], (((1,), (1,)), ((), ())), preferred_element_type=F32
            )
            kp = PREFIX - WIN + k * C + lax.broadcasted_iota(jnp.int32, (1, C), 1)
            ok = (kp <= pos) & (kp > pos - WIN)
            scores.append(jnp.where(ok, sc, MASKED))
            allow.append(ok)
            values.append(cb[:, HW:])
            kv = flat(kv_all[k])
            sc = lax.dot_general(
                q, kv[:, :HW], (((1,), (1,)), ((), ())), preferred_element_type=F32
            )
            j = lax.broadcasted_iota(jnp.int32, (1, N * R), 1)
            kp = PREFIX + offs[k] + j
            ok = (kp <= pos) & (kp > pos - WIN) & (j < lens[k])
            scores.append(jnp.where(ok, sc, MASKED))
            allow.append(ok)
            values.append(kv[:, HW:])
        top = functools.reduce(
            jnp.maximum, [jnp.max(v, axis=1, keepdims=True) for v in scores]
        )
        row_sum = jnp.zeros((R, 1), F32)
        acc = jnp.zeros((R, HW), F32)
        for sc, ok, vv in zip(scores, allow, values):
            w = jnp.where(ok, jnp.exp(sc - top), 0.0)
            row_sum = row_sum + jnp.sum(w, axis=1, keepdims=True)
            acc = acc + jnp.dot(w.astype(BF16), vv, preferred_element_type=F32)
        live = slot_c < own_len
        res = acc / jnp.where(live, row_sum, 1.0)
        hsnd[n] = jnp.where(live, res, 0.0).astype(BF16)

        @pl.when(d < N)
        def _():
            pltpu.make_async_remote_copy(
                src_ref=hsnd.at[n], dst_ref=ho.at[z], send_sem=hssem.at[n],
                recv_sem=r_h.at[z], device_id={"tp": n}, device_id_type=MESH,
            ).start()

        return carry

    lax.fori_loop(1, N + 1, attend, 0)
    ho[z] = hsnd[z]

    for j in range(NG):
        out_third(j)
    for j in range(NG):
        out_last(j)
    for k in zs:
        arrived(ho.at[k], r_h.at[k])

    CC = chunk_of(DC, 1024)

    for k in range(S):
        def cols(i, carry):
            cs = pl.ds(pl.multiple_of(i * CC, CC), CC)
            acc = jnp.zeros((R, CC), F32)
            for g in range(N):
                w = jnp.concatenate([og[k, kt, g, :, cs] for kt in range(T)], axis=0)
                acc = acc + jnp.dot(ho[g], w, preferred_element_type=F32).astype(BF16).astype(F32)
            proj[:, pl.ds(pl.multiple_of(k * DC + i * CC, 128), CC)] = acc
            return carry

        lax.fori_loop(0, DC // CC, cols, 0)

    def finish(i, carry):
        rows = pl.ds(pl.multiple_of(i * RB, RB), RB)
        v = proj[rows, :]
        inv = lax.rsqrt(jnp.sum(v * v, axis=1, keepdims=True) * (1.0 / D) + EPSILON)
        out_ref[rows, :] = (xbuf[b, rows, :].astype(F32) + v * inv * pgain[...]).astype(BF16)
        return carry

    lax.fori_loop(0, R // RB, finish, 0)

    for c in pending:
        c.wait_send()
    for k in zs:
        pltpu.make_async_remote_copy(
            src_ref=hsnd.at[k], dst_ref=ho.at[z], send_sem=hssem.at[k],
            recv_sem=r_h.at[z], device_id={"tp": k}, device_id_type=MESH,
        ).wait_send()


def shards(
    T, S, N,
    tokens, lengths, input_gain, query_proj, key_value, query_gain, key_gain,
    window_cache, output_proj, post_gain,
):
    R, D = tokens.shape
    HW = query_proj.shape[1]
    C = window_cache.shape[0]
    h = N // 2
    S2 = max(d for d in range(1, S + 1) if S % d == 0 and D % (16 * T * d) == 0)
    NC = max(d for d in (1, 2, 3) if D // (T * S2) % (16 * d) == 0)
    NG = max(d for d in (1, 2, 4) if N % d == 0)
    inv = np.power(ROPE_BASE, -2.0 * np.arange(HW // 2) / HW)
    freq = np.concatenate([inv, inv])[None, :].astype(np.float32)
    OR, DC = output_proj.shape[0] // T, output_proj.shape[1]
    Y = T // 2 - 1
    w_sends = 2 * NC * (1 + (S2 + Y) + (S2 - 1) * (Y + 1) + Y * S2)
    o_sends = (N - 1) + NG * ((S + Y) + Y * S + (S - 1) * (Y + 1) + 2 * (S - 1) * Y)
    sends = w_sends + o_sends + (h - 1) + (S - 1) + N * (S - 1) + 2 * h
    held = 3 * h * R * D * 2 + 6 * D * HW * 2 + 2 * S * C * HW * 2 + S * T * N * OR * DC * 2
    held += (6 + 2 * S) * N * R * HW * 2 + R * D * 4 + R * D * 2
    vm = pl.BlockSpec(memory_space=pltpu.VMEM)
    hb = pl.BlockSpec(memory_space=pltpu.HBM)
    dma = pltpu.SemaphoreType.DMA
    return pl.pallas_call(
        functools.partial(kernel, T, S, N, S2, NC, NG),
        out_shape=jax.ShapeDtypeStruct((R, D), BF16),
        in_specs=[pl.BlockSpec(memory_space=pltpu.SMEM), hb, hb, hb, hb, hb]
        + [hb, hb, vm, vm, vm],
        out_specs=vm,
        scratch_shapes=[
            pltpu.VMEM((D // 128, 128), F32),
            pltpu.VMEM((D // 128, 128), F32),
            pltpu.VMEM((1, D), F32),
            pltpu.VMEM((1, D), F32),
            pltpu.VMEM((h, R, HW), F32),
            pltpu.VMEM((h, R, HW), F32),
            pltpu.VMEM((h, R, D), BF16),
            pltpu.VMEM((h, R, D), BF16),
            pltpu.VMEM((2, D, HW), BF16),
            pltpu.VMEM((2, D, 2 * HW), BF16),
            pltpu.VMEM((S, C, 2 * HW), BF16),
            pltpu.VMEM((S, T, N, OR, DC), BF16),
            pltpu.VMEM((N, R, HW), BF16),
            pltpu.VMEM((S, N, R, 2 * HW), BF16),
            pltpu.VMEM((h, R, HW), BF16),
            pltpu.VMEM((h, R, 2 * HW), BF16),
            pltpu.VMEM((N, R, HW), BF16),
            pltpu.VMEM((N, R, HW), BF16),
            pltpu.VMEM((R, D), F32),
            dma((7,)), dma((sends,)), dma((N,)),
            dma((h,)), dma((S,)), dma((2, T, S2, NC)), dma((N,)), dma((2, S, T, NG)),
            dma((N,)), dma((N,)), dma((S, N)), dma((N,)), dma((2, NC)),
        ],
        compiler_params=pltpu.CompilerParams(
            collective_id=0, has_side_effects=True, vmem_limit_bytes=held + 10 * 2**20
        ),
    )(
        lengths, tokens, query_proj, key_value, window_cache, output_proj,
        input_gain.reshape(D // 128, 128), post_gain.reshape(D // 128, 128),
        query_gain[None, :], key_gain[None, :], jnp.asarray(freq),
    )


def solution(mesh):
    T, S, N = mesh.shape["tmpl"], mesh.shape["seq"], mesh.shape["tp"]
    return jax.shard_map(
        functools.partial(shards, T, S, N),
        mesh=mesh,
        in_specs=(
            P(("tmpl", "seq", "tp"), None),
            P("tmpl"),
            P(),
            P(None, "tp"),
            P(None, "tp"),
            P(),
            P(),
            P(("tmpl", "seq"), "tp"),
            P("tp", "seq"),
            P(),
        ),
        out_specs=P(("tmpl", "seq", "tp"), None),
        check_vma=False,
    )
```

```python
import functools

import jax
import jax.numpy as jnp
import numpy as np
from jax import lax
from jax.experimental import pallas as pl
from jax.experimental.pallas import tpu as pltpu
from jax.sharding import PartitionSpec as P

WIN = 1024
PREFIX = 32768
EPSILON = 1e-06
ROPE_BASE = 10000.0
QUERY_SCALE = 168.0 ** (-0.5)
MASKED = -1e30
F32 = jnp.float32
BF16 = jnp.bfloat16
MESH = pl.DeviceIdType.MESH


def chunk_of(width, limit):
    best = 128
    for c in range(128, limit + 1, 128):
        if width % c == 0:
            best = c
    return best


def flat(v):
    shape = (v.shape[0] * v.shape[1], v.shape[2])
    if v.shape[1] % 16 == 0:
        return v.reshape(shape)
    return v.astype(F32).reshape(shape).astype(v.dtype)


def kernel(
    T, S, N, S2, NC, NG,
    lengths, tokens, wq_hbm, wkv_hbm, cache_hbm, oproj_hbm,
    ig_hbm, pg_hbm, qgain, kgain, freq,
    out_ref,
    igs, pgs, igain, pgain, cos_t, sin_t, xbuf, nbuf, wq, wkv, cbuf, og, q_all, kv_all, q_snd, kv_snd, hsnd, ho, proj,
    lsem, ssem, hssem,
    r_x, r_c, r_w, r_oz, r_o, r_q, r_kv, r_kvx, r_h, r_own,
):
    t, s, z = lax.axis_index("tmpl"), lax.axis_index("seq"), lax.axis_index("tp")
    h = N // 2
    p, b = z // h, z % h
    zp = (z + h) % N
    R, D = tokens.shape
    HW = wq_hbm.shape[1]
    C = cache_hbm.shape[0]
    DE = D // (T * S2)
    OR = oproj_hbm.shape[0] // T
    DC = oproj_hbm.shape[1]
    tc = t + 1 - 2 * (t % 2)
    par = t % 2
    ys = [(t + 2 * k) % T for k in range(1, T // 2)]
    xs = [(s + k) % S for k in range(1, S)]
    sg, sb = (s // S2) * S2, s % S2
    x2 = [(sb + k) % S2 for k in range(1, S2)]
    zs = [(z + k) % N for k in range(1, N)]

    pending = []

    def queue(src, dst, rsem, dev):
        c = pltpu.make_async_remote_copy(
            src_ref=src, dst_ref=dst, send_sem=ssem.at[len(pending)], recv_sem=rsem,
            device_id=dev, device_id_type=MESH,
        )
        pending.append(c)
        return c

    def send(src, dst, rsem, dev):
        queue(src, dst, rsem, dev).start()

    def arrived(dst, rsem):
        pltpu.make_async_remote_copy(
            src_ref=dst, dst_ref=dst, send_sem=ssem.at[0], recv_sem=rsem,
            device_id={"tp": zp}, device_id_type=MESH,
        ).wait_recv()

    loc = [
        pltpu.make_async_copy(tokens, xbuf.at[b], lsem.at[0]),
        pltpu.make_async_copy(wq_hbm, wq.at[0], lsem.at[1]),
        pltpu.make_async_copy(wkv_hbm, wkv.at[0], lsem.at[2]),
        pltpu.make_async_copy(cache_hbm, cbuf.at[s], lsem.at[3]),
        pltpu.make_async_copy(
            oproj_hbm.at[pl.ds(pl.multiple_of(t * OR, OR), OR)], og.at[s, t, z], lsem.at[4]
        ),
        pltpu.make_async_copy(ig_hbm, igs, lsem.at[5]),
        pltpu.make_async_copy(pg_hbm, pgs, lsem.at[6]),
    ]
    for c in loc:
        c.start()

    barrier = pltpu.get_barrier_semaphore()
    peers = (
        [{"tp": k} for k in zs] + [{"seq": k} for k in xs]
        + [{"tmpl": k} for k in ys] + [{"tmpl": tc}]
    )
    for dev in peers:
        pl.semaphore_signal(barrier, inc=1, device_id=dev, device_id_type=MESH)
    pl.semaphore_wait(barrier, len(peers))

    DN = DE // NC

    def piece(e_t, e_s, c):
        return pl.ds(pl.multiple_of((e_t * S2 + e_s) * DE + c * DN, DN), DN)

    wset = [
        (c, a, src, buf)
        for c in range(NC)
        for a, src, buf in ((1, wkv_hbm, wkv), (0, wq_hbm, wq))
    ]
    w_first = [
        queue(
            src.at[piece(t, sb, c)], buf.at[1, piece(t, sb, c)],
            r_own.at[a, c], {"tp": zp},
        )
        for c, a, src, buf in wset
    ]
    rows_first = [
        queue(tokens, xbuf.at[b], r_x.at[b], {"tp": p * h + (b + k) % h})
        for k in range(1, h)
    ]

    out_first = [
        queue(
            oproj_hbm.at[pl.ds(pl.multiple_of(t * OR, OR), OR)], og.at[s, t, z],
            r_oz.at[z], {"tp": k},
        )
        for k in zs
    ]

    @pl.when(par == 0)
    def _():
        for c in w_first + out_first + rows_first:
            c.start()

    @pl.when(par == 1)
    def _():
        for c in rows_first + w_first + out_first:
            c.start()

    for k in xs:
        send(cache_hbm, cbuf.at[s], r_c.at[s], {"seq": k})

    GN = N // NG
    gz, zl = z // GN, z % GN
    OH = OR // 2

    def op_full(ps, pt, g):
        return og.at[ps, pt, pl.ds(g * GN, GN)]

    def op_half(ps, pt, g, f):
        return og.at[ps, pt, pl.ds(g * GN, GN), pl.ds(f * OH, OH)]

    def out_own(j):
        g = (gz + j) % NG
        for k in range(1 if j == 0 else 0, GN):
            n = g * GN + (zl + k) % GN
            arrived(og.at[s, t, n], r_oz.at[n])
        pc = op_full(s, t, g)
        for k in xs:
            send(pc, pc, r_o.at[0, s, t, g], {"seq": k})
        for k in ys:
            send(pc, pc, r_o.at[0, s, t, g], {"tmpl": k})
        send(pc, pc, r_o.at[0, s, t, g], {"tmpl": tc})

    def out_second(j):
        g = (gz + j) % NG
        for kt in ys:
            pc = op_full(s, kt, g)
            arrived(pc, r_o.at[0, s, kt, g])
            hf = op_half(s, kt, g, 0)
            for k in xs:
                send(hf, hf, r_o.at[0, s, kt, g], {"seq": k})
            send(pc, pc, r_o.at[0, s, kt, g], {"tmpl": tc})
        for ks in xs:
            pc = op_full(ks, t, g)
            arrived(pc, r_o.at[0, ks, t, g])
            hf = op_half(ks, t, g, 1)
            for k in ys:
                send(hf, hf, r_o.at[1, ks, t, g], {"tmpl": k})
            send(pc, pc, r_o.at[0, ks, t, g], {"tmpl": tc})

    def out_third(j):
        g = (gz + j) % NG
        for ks in xs:
            for kt in ys:
                for f in range(2):
                    hf = op_half(ks, kt, g, f)
                    arrived(hf, r_o.at[f, ks, kt, g])
                    send(hf, hf, r_o.at[f, ks, kt, g], {"tmpl": tc})

    def out_last(j):
        g = (gz + j) % NG
        for i in range(S):
            for m in range(T // 2):
                ks, kt = (s + i) % S, (tc + 2 * m) % T
                if i and m:
                    for f in range(2):
                        arrived(op_half(ks, kt, g, f), r_o.at[f, ks, kt, g])
                else:
                    arrived(op_full(ks, kt, g), r_o.at[0, ks, kt, g])

    loc[4].wait()
    if GN == 1:
        out_own(0)

    lens = [lengths[k] for k in range(S)]
    offs = []
    total = jnp.int32(0)
    for k in range(S):
        offs.append(total)
        total = total + lens[k]
    own_off = jnp.int32(0)
    own_len = jnp.int32(0)
    for k in range(S):
        own_off = own_off + jnp.where(s == k, offs[k], 0)
        own_len = own_len + jnp.where(s == k, lens[k], 0)

    RB = 16 if R % 16 == 0 else 8
    KC = chunk_of(D, 1024)

    def norm_rows(slot):
        def body(i, carry):
            rows = pl.ds(pl.multiple_of(i * RB, RB), RB)
            v = xbuf[slot, rows, :].astype(F32)
            inv = lax.rsqrt(jnp.sum(v * v, axis=1, keepdims=True) * (1.0 / D) + EPSILON)
            nbuf[slot, rows, :] = (v * inv * igain[...]).astype(BF16)
            return carry

        lax.fori_loop(0, R // RB, body, 0)

    def head_norm(v, gain):
        inv = lax.rsqrt(jnp.mean(v * v, axis=1, keepdims=True) + EPSILON)
        return v * inv * gain

    def project(slots, j):
        def body(i, acc):
            ks = pl.ds(pl.multiple_of(i * KC, KC), KC)
            xv = [nbuf[slot, :, ks] for slot in slots]
            xv = jnp.concatenate(xv, axis=0) if len(slots) > 1 else xv[0]
            return (
                acc[0] + jnp.dot(xv, wq[j, ks, :], preferred_element_type=F32),
                acc[1] + jnp.dot(xv, wkv[j, ks, :], preferred_element_type=F32),
            )

        M = R * len(slots)
        qr, kv = lax.fori_loop(
            0, D // KC, body, (jnp.zeros((M, HW), F32), jnp.zeros((M, 2 * HW), F32))
        )
        out = []
        for i, slot in enumerate(slots):
            co, si = cos_t[slot], sin_t[slot]
            rows = slice(i * R, (i + 1) * R)

            def rope(u):
                return u * co + pltpu.roll(u, HW // 2, 1) * si

            q = (rope(head_norm(qr[rows], qgain[...])) * QUERY_SCALE).astype(BF16)
            k = rope(head_norm(kv[rows, :HW], kgain[...])).astype(BF16)
            out.append((q, jnp.concatenate([k, kv[rows, HW:].astype(BF16)], axis=1)))
        return out

    def own_head(slot):
        q, kv = project([slot], 0)[0]
        n = p * h + slot
        q_all[n] = q
        kv_all[s, n] = kv
        for k in xs:
            send(kv_all.at[s, n], kv_all.at[s, n], r_kvx.at[s, n], {"seq": k})

    def other_head(slot, q, kv):
        n = p * h + slot
        q_snd[slot] = q
        kv_snd[slot] = kv
        send(kv_snd.at[slot], kv_all.at[s, n], r_kv.at[n], {"tp": zp})
        send(q_snd.at[slot], q_all.at[n], r_q.at[n], {"tp": zp})

    loc[5].wait()
    loc[6].wait()
    for k in range(D // 128):
        igain[0:1, k * 128 : (k + 1) * 128] = igs[k : k + 1, :]
        pgain[0:1, k * 128 : (k + 1) * 128] = pgs[k : k + 1, :]
    lane = lax.broadcasted_iota(jnp.int32, (R, HW), 1)
    for k in range(h):
        row = lax.broadcasted_iota(jnp.int32, (R, HW), 0)
        angle = (PREFIX + own_off + (p * h + k) * R + row).astype(F32) * freq[...]
        cos_t[k] = jnp.cos(angle)
        sine = jnp.sin(angle)
        sin_t[k] = jnp.where(lane < HW // 2, -sine, sine)
    loc[0].wait()
    norm_rows(b)
    loc[1].wait()
    loc[2].wait()
    own_head(b)

    def w_own(c, a, src, buf):
        pc = buf.at[1, piece(t, sb, c)]
        arrived(pc, r_own.at[a, c])
        for k in x2:
            send(pc, pc, r_w.at[a, t, sb, c], {"seq": sg + k})
        for k in ys:
            send(pc, pc, r_w.at[a, t, sb, c], {"tmpl": k})
        send(pc, pc, r_w.at[a, t, sb, c], {"tmpl": tc})

    def w_x(c, a, src, buf):
        for k2 in x2:
            pc = buf.at[1, piece(t, k2, c)]
            arrived(pc, r_w.at[a, t, k2, c])
            for k in ys:
                send(pc, pc, r_w.at[a, t, k2, c], {"tmpl": k})
            send(pc, pc, r_w.at[a, t, k2, c], {"tmpl": tc})

    def w_y(c, a, src, buf):
        for k in ys:
            for k2 in range(S2):
                ks = (sb + k2) % S2
                pc = buf.at[1, piece(k, ks, c)]
                arrived(pc, r_w.at[a, k, ks, c])
                send(pc, pc, r_w.at[a, k, ks, c], {"tmpl": tc})

    for i in range(NC + 1):
        if i < NC:
            for w in wset[2 * i : 2 * i + 2]:
                w_own(*w)
        if i == 0 and GN == 1:
            out_second(0)
        if i > 0:
            for w in wset[2 * i - 2 : 2 * i]:
                w_x(*w)
    for j in range(1 if GN == 1 else 0, NG):
        out_own(j)

    for w in wset:
        w_y(*w)

    for k in range(1, h):
        slot = (b + k) % h
        arrived(xbuf.at[slot], r_x.at[slot])
        norm_rows(slot)
        own_head(slot)
    for c, a, src, buf in wset:
        for k in range(T // 2):
            kt = (1 - par) + 2 * k
            for ks in range(S2):
                arrived(buf.at[1, piece(kt, ks, c)], r_w.at[a, kt, ks, c])
    if R % 16 == 0:
        done = project(list(range(h)), 1)
    else:
        done = [project([k], 1)[0] for k in range(h)]
    for k in range(h):
        other_head(k, *done[k])

    op = 1 - p
    for i in range(h):
        n = op * h + i
        arrived(kv_all.at[s, n], r_kv.at[n])
        for k in xs:
            send(kv_all.at[s, n], kv_all.at[s, n], r_kvx.at[s, n], {"seq": k})
    for i in range(h):
        n = op * h + i
        arrived(q_all.at[n], r_q.at[n])
    for j in range(1 if GN == 1 else 0, NG):
        out_second(j)
    loc[3].wait()
    for k in xs:
        arrived(cbuf.at[k], r_c.at[k])
        for n in range(N):
            arrived(kv_all.at[k, n], r_kvx.at[k, n])

    def attend(d, carry):
        n = lax.rem(z + d, N)
        q = q_all[n]
        slot_c = n * R + lax.broadcasted_iota(jnp.int32, (R, 1), 0)
        pos = PREFIX + own_off + slot_c
        scores, allow, values = [], [], []
        for k in range(S):
            cb = cbuf[k]
            sc = lax.dot_general(
                q, cb[:, :HW], (((1,), (1,)), ((), ())), preferred_element_type=F32
            )
            kp = PREFIX - WIN + k * C + lax.broadcasted_iota(jnp.int32, (1, C), 1)
            ok = (kp <= pos) & (kp > pos - WIN)
            scores.append(jnp.where(ok, sc, MASKED))
            allow.append(ok)
            values.append(cb[:, HW:])
            kv = flat(kv_all[k])
            sc = lax.dot_general(
                q, kv[:, :HW], (((1,), (1,)), ((), ())), preferred_element_type=F32
            )
            j = lax.broadcasted_iota(jnp.int32, (1, N * R), 1)
            kp = PREFIX + offs[k] + j
            ok = (kp <= pos) & (kp > pos - WIN) & (j < lens[k])
            scores.append(jnp.where(ok, sc, MASKED))
            allow.append(ok)
            values.append(kv[:, HW:])
        top = functools.reduce(
            jnp.maximum, [jnp.max(v, axis=1, keepdims=True) for v in scores]
        )
        row_sum = jnp.zeros((R, 1), F32)
        acc = jnp.zeros((R, HW), F32)
        for sc, ok, vv in zip(scores, allow, values):
            w = jnp.where(ok, jnp.exp(sc - top), 0.0)
            row_sum = row_sum + jnp.sum(w, axis=1, keepdims=True)
            acc = acc + jnp.dot(w.astype(BF16), vv, preferred_element_type=F32)
        live = slot_c < own_len
        res = acc / jnp.where(live, row_sum, 1.0)
        hsnd[n] = jnp.where(live, res, 0.0).astype(BF16)

        @pl.when(d < N)
        def _():
            pltpu.make_async_remote_copy(
                src_ref=hsnd.at[n], dst_ref=ho.at[z], send_sem=hssem.at[n],
                recv_sem=r_h.at[z], device_id={"tp": n}, device_id_type=MESH,
            ).start()

        return carry

    lax.fori_loop(1, N + 1, attend, 0)
    ho[z] = hsnd[z]

    for j in range(NG):
        out_third(j)
    for j in range(NG):
        out_last(j)
    for k in zs:
        arrived(ho.at[k], r_h.at[k])

    CC = chunk_of(DC, 1024)

    for k in range(S):
        def cols(i, carry):
            cs = pl.ds(pl.multiple_of(i * CC, CC), CC)
            acc = jnp.zeros((R, CC), F32)
            for g in range(N):
                w = jnp.concatenate([og[k, kt, g, :, cs] for kt in range(T)], axis=0)
                acc = acc + jnp.dot(ho[g], w, preferred_element_type=F32).astype(BF16).astype(F32)
            proj[:, pl.ds(pl.multiple_of(k * DC + i * CC, 128), CC)] = acc
            return carry

        lax.fori_loop(0, DC // CC, cols, 0)

    def finish(i, carry):
        rows = pl.ds(pl.multiple_of(i * RB, RB), RB)
        v = proj[rows, :]
        inv = lax.rsqrt(jnp.sum(v * v, axis=1, keepdims=True) * (1.0 / D) + EPSILON)
        out_ref[rows, :] = (xbuf[b, rows, :].astype(F32) + v * inv * pgain[...]).astype(BF16)
        return carry

    lax.fori_loop(0, R // RB, finish, 0)

    for c in pending:
        c.wait_send()
    for k in zs:
        pltpu.make_async_remote_copy(
            src_ref=hsnd.at[k], dst_ref=ho.at[z], send_sem=hssem.at[k],
            recv_sem=r_h.at[z], device_id={"tp": k}, device_id_type=MESH,
        ).wait_send()


def shards(
    T, S, N,
    tokens, lengths, input_gain, query_proj, key_value, query_gain, key_gain,
    window_cache, output_proj, post_gain,
):
    R, D = tokens.shape
    HW = query_proj.shape[1]
    C = window_cache.shape[0]
    h = N // 2
    S2 = max(d for d in range(1, S + 1) if S % d == 0 and D % (16 * T * d) == 0)
    NC = max(d for d in (1, 2, 3, 6) if D // (T * S2) % (16 * d) == 0)
    NG = max(d for d in (1, 2, 4) if N % d == 0)
    inv = np.power(ROPE_BASE, -2.0 * np.arange(HW // 2) / HW)
    freq = np.concatenate([inv, inv])[None, :].astype(np.float32)
    OR, DC = output_proj.shape[0] // T, output_proj.shape[1]
    Y = T // 2 - 1
    w_sends = 2 * NC * (1 + (S2 + Y) + (S2 - 1) * (Y + 1) + Y * S2)
    o_sends = (N - 1) + NG * ((S + Y) + Y * S + (S - 1) * (Y + 1) + 2 * (S - 1) * Y)
    sends = w_sends + o_sends + (h - 1) + (S - 1) + N * (S - 1) + 2 * h
    held = 3 * h * R * D * 2 + 6 * D * HW * 2 + 2 * S * C * HW * 2 + S * T * N * OR * DC * 2
    held += (6 + 2 * S) * N * R * HW * 2 + R * D * 4 + R * D * 2
    vm = pl.BlockSpec(memory_space=pltpu.VMEM)
    hb = pl.BlockSpec(memory_space=pltpu.HBM)
    dma = pltpu.SemaphoreType.DMA
    return pl.pallas_call(
        functools.partial(kernel, T, S, N, S2, NC, NG),
        out_shape=jax.ShapeDtypeStruct((R, D), BF16),
        in_specs=[pl.BlockSpec(memory_space=pltpu.SMEM), hb, hb, hb, hb, hb]
        + [hb, hb, vm, vm, vm],
        out_specs=vm,
        scratch_shapes=[
            pltpu.VMEM((D // 128, 128), F32),
            pltpu.VMEM((D // 128, 128), F32),
            pltpu.VMEM((1, D), F32),
            pltpu.VMEM((1, D), F32),
            pltpu.VMEM((h, R, HW), F32),
            pltpu.VMEM((h, R, HW), F32),
            pltpu.VMEM((h, R, D), BF16),
            pltpu.VMEM((h, R, D), BF16),
            pltpu.VMEM((2, D, HW), BF16),
            pltpu.VMEM((2, D, 2 * HW), BF16),
            pltpu.VMEM((S, C, 2 * HW), BF16),
            pltpu.VMEM((S, T, N, OR, DC), BF16),
            pltpu.VMEM((N, R, HW), BF16),
            pltpu.VMEM((S, N, R, 2 * HW), BF16),
            pltpu.VMEM((h, R, HW), BF16),
            pltpu.VMEM((h, R, 2 * HW), BF16),
            pltpu.VMEM((N, R, HW), BF16),
            pltpu.VMEM((N, R, HW), BF16),
            pltpu.VMEM((R, D), F32),
            dma((7,)), dma((sends,)), dma((N,)),
            dma((h,)), dma((S,)), dma((2, T, S2, NC)), dma((N,)), dma((2, S, T, NG)),
            dma((N,)), dma((N,)), dma((S, N)), dma((N,)), dma((2, NC)),
        ],
        compiler_params=pltpu.CompilerParams(
            collective_id=0, has_side_effects=True, vmem_limit_bytes=67043328 - 2 * R * D * 2
        ),
    )(
        lengths, tokens, query_proj, key_value, window_cache, output_proj,
        input_gain.reshape(D // 128, 128), post_gain.reshape(D // 128, 128),
        query_gain[None, :], key_gain[None, :], jnp.asarray(freq),
    )


def solution(mesh):
    T, S, N = mesh.shape["tmpl"], mesh.shape["seq"], mesh.shape["tp"]
    return jax.shard_map(
        functools.partial(shards, T, S, N),
        mesh=mesh,
        in_specs=(
            P(("tmpl", "seq", "tp"), None),
            P("tmpl"),
            P(),
            P(None, "tp"),
            P(None, "tp"),
            P(),
            P(),
            P(("tmpl", "seq"), "tp"),
            P("tp", "seq"),
            P(),
        ),
        out_specs=P(("tmpl", "seq", "tp"), None),
        check_vma=False,
    )
```
